32 devices in a mesh: tm: 4 (over y, x), dp: 8 (over z, core).
Axes of the slice: x: 2, y: 2, z: 4, core: 2. Of those that a mesh axis runs over, the one named last changes fastest.
Arguments:
- features: bfloat16 [8, 16, 2, 8, 256], P('dp', 'tm'), may hold values from -6 to 6
- upstream: bfloat16 [8, 16, 4, 16, 128], P('dp', 'tm'), may hold values from -6 to 6
- weight_one: bfloat16 [3, 3, 3, 256, 128], replicated, may hold values from -0.078125 to 0.078125
- weight_two: bfloat16 [3, 3, 3, 128, 128], replicated, may hold values from -0.109375 to 0.109375
Outputs:
- feature_grad: bfloat16 [8, 16, 2, 8, 256], P('dp', 'tm')
- grad_one: float32 [3, 3, 3, 256, 128], P(None, None, None, 'dp')
- grad_two: float32 [3, 3, 3, 128, 128], P(None, None, None, 'dp')
The draws below stay inside these ranges and needn't reach their ends.
All inputs are finite; a program needn't handle non-finite values.
Results may differ from the reference program's by a relative error of at most 0.0049.
Values may be sent and summed in bfloat16 or wider, within the bound.
No kernel may reach another device: no remote copies, remote signals or barrier semaphores. Data moves between devices by JAX's collectives and lax.ppermute only.
A program may use at most 64 MiB of HBM per device.

```python
import jax
import jax.numpy as jnp
from jax import lax

CIN = 256
COUT = 128
HI = 2
WI = 8
HO = 4
WO = 16
CLIPS = 8
FRAMES = 16


def level_of(key, shape, split, least, largest):
    level, own = 1.0, jax.random.fold_in(key, 6)
    for dim, parts in split:
        heights = jnp.exp(jax.random.uniform(jax.random.fold_in(own, dim), (parts,), jnp.float32, least / len(split), largest / len(split)))
        level = level * jnp.repeat(heights, shape[dim] // parts).reshape([-1 if axis == dim else 1 for axis in range(len(shape))])
    return level


def bell_draw(own_key, shape, deviation, limit, shards=(), kind=jnp.bfloat16):
    array = deviation * jax.random.normal(own_key, shape, jnp.float32)
    if shards:
        array = array * level_of(own_key, shape, shards, -0.22, 0.18)
    return jnp.clip(array, -limit, limit).astype(kind)


def setup_inputs(seed: int = 0) -> dict:
    arg_keys = jax.random.split(jax.random.key(seed), 5)
    return {
        "features": bell_draw(arg_keys[0], (CLIPS, FRAMES, HI, WI, CIN), 1.0, 6.0, ((0, 8), (1, 4))),
        "upstream": bell_draw(arg_keys[1], (CLIPS, FRAMES, HO, WO, COUT), 1.0, 6.0, ((0, 8), (1, 4))),
        "weight_one": bell_draw(arg_keys[2], (3, 3, 3, CIN, COUT), (27 * CIN) ** -0.5, 0.078125),
        "weight_two": bell_draw(arg_keys[3], (3, 3, 3, COUT, COUT), (27 * COUT) ** -0.5, 0.109375),
    }


def upsample(values):
    return jnp.repeat(jnp.repeat(values, 2, axis=2), 2, axis=3)

def forward_conv(padded, kernel):
    return lax.conv_general_dilated(padded, kernel, (1, 1, 1), 'VALID', dimension_numbers=('NDHWC', 'DHWIO', 'NDHWC'), preferred_element_type=jnp.float32)

def kernel_grad(padded, cotangent):
    return lax.conv_general_dilated(padded, cotangent, (1, 1, 1), 'VALID', dimension_numbers=('CDHWN', 'IDHWO', 'DHWNC'), preferred_element_type=jnp.float32)

def data_grad(cotangent, kernel):
    return lax.conv_general_dilated(cotangent, kernel[::-1, ::-1, ::-1], (1, 1, 1), [(2, 2), (2, 2), (2, 2)], dimension_numbers=('NDHWC', 'DHWOI', 'NDHWC'), preferred_element_type=jnp.float32)

def pad_causal(values):
    return jnp.pad(values, ((0, 0), (2, 0), (1, 1), (1, 1), (0, 0)))

def silu_slope(pre):
    sigma = jax.nn.sigmoid(pre)
    return sigma * (1.0 + pre * (1.0 - sigma))

def pool_pairs(values):
    shape = values.shape
    return values.reshape(shape[0], shape[1], shape[2] // 2, 2, shape[3] // 2, 2, shape[4]).sum(axis=(3, 5))

def reference(features, upstream, weight_one, weight_two):
    count = upstream.shape[0] * upstream.shape[1] * upstream.shape[2] * upstream.shape[3]
    factor = 1.0 / count ** 0.5

    def one_clip(pair):
        feats, cotangent = pair
        cotangent = cotangent[None]
        padded = pad_causal(upsample(feats[None]))
        pre = forward_conv(padded, weight_one)
        hidden = jax.nn.silu(pre).astype(jnp.bfloat16)
        grad_second = kernel_grad(pad_causal(hidden), cotangent)
        back = data_grad(cotangent, weight_two)[:, 2:, 1:-1, 1:-1]
        dpre = (back * silu_slope(pre)).astype(jnp.bfloat16)
        grad_first = kernel_grad(padded, dpre)
        up_grad = data_grad(dpre, weight_one)[:, 2:, 1:-1, 1:-1]
        return (pool_pairs(up_grad).astype(jnp.bfloat16)[0], grad_first, grad_second)
    results = lax.map(one_clip, (features, upstream))
    return (results[0], lax.optimization_barrier(jnp.sum(results[1], axis=0)) * factor, lax.optimization_barrier(jnp.sum(results[2], axis=0)) * factor)
```

```python
import math

import jax
import jax.numpy as jnp
from jax import lax
from jax.experimental import pallas as pl
from jax.experimental.pallas import tpu as pltpu
from jax.sharding import PartitionSpec as P

F32, BF16 = jnp.float32, jnp.bfloat16


def swap(value, axis, hop, stride=1):
    size = lax.axis_size(axis)
    return lax.ppermute(value, axis, [(i, i ^ (hop * stride)) for i in range(size)])


def call(body, out_shape, name, scratch=(), flops=0):
    return pl.pallas_call(
        body,
        out_shape=out_shape,
        scratch_shapes=list(scratch),
        name=name,
        cost_estimate=pl.CostEstimate(flops=flops, transcendentals=0, bytes_accessed=0) if flops else None,
    )


def rows_of(value):
    return value.reshape(-1, value.shape[-1])


def move_down(value, fill_at):
    shape = value.shape
    flat = value.reshape(-1, shape[-2], shape[-1])
    by = 1 if fill_at == 0 else shape[-2] - 1
    turned = pltpu.roll(flat, by, 1)
    place = lax.broadcasted_iota(jnp.int32, turned.shape, 1)
    return jnp.where(place == fill_at, 0.0, turned).reshape(shape)


def pack_kernel(feats_ref, ups_ref, out_ref, wide):
    half = out_ref.shape[-1]
    low = feats_ref.shape[1]
    ins = feats_ref.shape[2] // half
    for part in range(ins):
        out_ref[:, part * low : (part + 1) * low, :] = feats_ref[:, :, part * half : (part + 1) * half]
    frames, ho, wo, _ = ups_ref.shape
    wide[...] = ups_ref[...].reshape(frames * ho, wo, half).astype(F32)
    even = wide[:, pl.ds(0, wo // 2, stride=2), :]
    odd = wide[:, pl.ds(1, wo // 2, stride=2), :]
    both = jnp.concatenate([even, odd], axis=1)
    out_ref[:, ins * low :, :] = both.reshape(frames, ho * wo, half).astype(BF16)


def main_kernel(dims, blocks, w1_ref, w2_ref, keep_ref, send_ref, dbox_ref, xs, uc, ht, ft, g1, g2):
    tm, dp, hi, wi, chunk = dims
    ho, wo = 2 * hi, 2 * wi
    low = hi * wi
    frames = blocks[0].shape[0]
    total = frames * tm
    cin, cout = w1_ref.shape[1], w1_ref.shape[2]
    parts = cin // cout
    me = lax.axis_index("tm")
    mine = lax.axis_index("dp")
    core, far = lax.rem(mine, 2), lax.div(mine, 2)

    xs[: 2 * low] = jnp.zeros((2 * low, cin), BF16)
    uc[:, total:] = jnp.zeros((3, 2) + uc.shape[2:], BF16)
    uc[:, :, 0] = jnp.zeros((3, total + 2) + uc.shape[3:], BF16)
    uc[:, :, ho + 1] = jnp.zeros((3, total + 2) + uc.shape[3:], BF16)
    for hop, block in enumerate(blocks):
        start = (me ^ hop) * frames
        feats = jnp.concatenate(
            [rows_of(block[:, part * low : (part + 1) * low, :]) for part in range(parts)], axis=1
        )
        xs[pl.ds(pl.multiple_of((start + 2) * low, low), frames * low), :] = feats
        ups = block[:, parts * low :, :].reshape(frames, ho, 2, wi, cout)
        wide = ups.astype(F32)
        even, odd = wide[:, :, 0], wide[:, :, 1]
        after = move_down(even, wi - 1)
        before = move_down(odd, 0)
        where = (pl.ds(start, frames), slice(1, ho + 1))
        uc[(0,) + where] = jnp.concatenate([odd, after], axis=2).astype(BF16)
        uc[(1,) + where] = block[:, parts * low :, :].reshape(frames, ho, wo, cout)
        uc[(2,) + where] = jnp.concatenate([before, even], axis=2).astype(BF16)

    by_row = []
    for b in range(3):
        sums = None
        for a in range(3):
            weight = jnp.concatenate([w1_ref[a * 9 + b * 3 + e] for e in range(3)], axis=1)
            term = jnp.dot(xs[a * low : (a + total) * low, :], weight, preferred_element_type=F32)
            sums = term if sums is None else sums + term
        by_row.append(sums.reshape(total, hi, wi, 3 * cout))
    zero = jnp.zeros((total, wi, 3 * cout), F32)
    pre_rows = []
    for row in range(hi):
        up = by_row[0][:, row - 1] if row else zero
        down = by_row[2][:, row + 1] if row + 1 < hi else zero
        pre_rows.append(up + by_row[1][:, row] + by_row[2][:, row])
        pre_rows.append(by_row[0][:, row] + by_row[1][:, row] + down)
    sums = jnp.stack(pre_rows, axis=1)
    first, middle, last = (sums[..., e * cout : (e + 1) * cout] for e in range(3))
    even = move_down(first, 0) + middle + last
    odd = first + middle + move_down(last, wi - 1)
    pre = jnp.concatenate([even, odd], axis=2)
    sigma = 1.0 / (1.0 + jnp.exp(-pre))
    hidden = pre * sigma
    slope = sigma * (1.0 + pre * (1.0 - sigma))
    ht[...] = rows_of(hidden).T.astype(BF16)
    ft[...] = xs[2 * low :, :].astype(F32).T.astype(BF16)

    back = None
    for a in range(3):
        for b in range(3):
            ups = jnp.concatenate(
                [rows_of(uc[e, 2 - a : 2 - a + total, 2 - b : 2 - b + ho]) for e in range(3)], axis=1
            )
            weight = jnp.concatenate([w2_ref[a * 9 + b * 3 + e] for e in range(3)], axis=1)
            term = lax.dot_general(ups, weight, (((1,), (1,)), ((), ())), preferred_element_type=F32)
            back = term if back is None else back + term
    dpre = (back.reshape(slope.shape) * slope).astype(BF16).astype(F32)
    even, odd = dpre[:, :, :wi], dpre[:, :, wi:]
    columns = (odd + move_down(even, wi - 1), even + odd, move_down(odd, 0) + even)
    for e in range(3):
        col = columns[e]
        for b in range(3):
            picked = []
            for row in range(hi):
                one, two = 2 * row + 1 - b, 2 * row + 2 - b
                value = None
                for at in (one, two):
                    if 0 <= at < ho:
                        value = col[:, at] if value is None else value + col[:, at]
                picked.append(value)
            box = jnp.concatenate(picked, axis=1)
            dbox_ref[b * 3 + e, :total] = box.astype(BF16)
    dbox_ref[:, total:] = jnp.zeros((9, 2, low, cout), BF16)

    far_size = dp // 2
    tall, short = cin // dp, cout // dp
    for j in range(chunk):
        tap = jnp.minimum(me * chunk + j, 26)
        a, rest = lax.div(tap, 9), lax.rem(tap, 9)
        b, e = lax.div(rest, 3), lax.rem(rest, 3)
        boxes = rows_of(dbox_ref[rest, pl.ds(2 - a, total)])
        g1[j] = jnp.dot(ft[...], boxes, preferred_element_type=F32)
        ups = rows_of(uc[e, pl.ds(2 - a, total), pl.ds(2 - b, ho)])
        g2[j] = jnp.dot(ht[...], ups, preferred_element_type=F32)
    for hop in range(far_size):
        for ref, side in ((keep_ref, core), (send_ref, 1 - core)):
            at = (far ^ hop) * 2 + side
            ref[hop, :, :tall] = g1[:, pl.ds(pl.multiple_of(at * tall, tall), tall)].astype(ref.dtype)
            ref[hop, :, tall:] = g2[:, pl.ds(pl.multiple_of(at * short, short), short)].astype(ref.dtype)


def input_grad_kernel(frames, dbox_ref, w1_ref, out_ref):
    start = lax.axis_index("tm") * frames
    total = None
    for a in range(3):
        for b in range(3):
            boxes = jnp.concatenate(
                [rows_of(dbox_ref[b * 3 + e, pl.ds(start + 2 - a, frames)]) for e in range(3)], axis=1
            )
            weight = jnp.concatenate([w1_ref[a * 9 + b * 3 + e] for e in range(3)], axis=1)
            term = lax.dot_general(boxes, weight, (((1,), (1,)), ((), ())), preferred_element_type=F32)
            total = term if total is None else total + term
    out_ref[...] = total.astype(BF16)


def pair_kernel(keep_ref, recv_ref, own_ref, *send_refs):
    own_ref[...] = keep_ref[0] + recv_ref[0].astype(F32)
    for hop, ref in enumerate(send_refs, 1):
        ref[...] = (keep_ref[hop] + recv_ref[hop].astype(F32)).astype(BF16)


def sum_kernel(factor, own_ref, *refs):
    *recv_refs, out_ref = refs
    total = own_ref[...]
    for ref in recv_refs:
        total += ref[...].astype(F32)
    out_ref[...] = (total * factor).astype(BF16)


def spread_kernel(tall, *refs):
    *in_refs, one_ref, two_ref = refs
    me = lax.axis_index("tm")
    chunk = in_refs[0].shape[0]
    taps = one_ref.shape[0]
    for hop, ref in enumerate(in_refs):
        for j in range(chunk):
            tap = (me ^ hop) * chunk + j

            @pl.when(tap < taps)
            def _():
                one_ref[tap] = ref[j, :tall].astype(F32)
                two_ref[tap] = ref[j, tall:].astype(F32)


def on_device(features, upstream, weight_one, weight_two):
    clips, frames, hi, wi, cin = features.shape
    ho, wo, cout = upstream.shape[2:]
    tm, dp = lax.axis_size("tm"), lax.axis_size("dp")
    taps = 27
    chunk = -(-taps // tm)
    total = frames * tm
    low, high = hi * wi, ho * wo
    far_size = dp // 2
    tall, short = cin // dp, cout // dp
    shape = jax.ShapeDtypeStruct
    w1 = weight_one.reshape(taps, cin, cout)
    w2 = weight_two.reshape(taps, cout, cout)

    packed = call(
        pack_kernel,
        shape((frames, low * (cin // cout) + high, cout), BF16),
        "pack",
        [pltpu.VMEM((frames * ho, wo, cout), F32)],
    )(features.reshape(frames, low, cin), upstream.reshape(frames, ho, wo, cout))
    blocks = [packed] + [swap(packed, "tm", hop) for hop in range(1, tm)]

    def main_body(*refs):
        main_kernel((tm, dp, hi, wi, chunk), refs[:tm], *refs[tm:])

    keep, send, dbox = call(
        main_body,
        (
            shape((far_size, chunk, tall + short, cout), F32),
            shape((far_size, chunk, tall + short, cout), BF16),
            shape((9, total + 2, low, cout), BF16),
        ),
        "main",
        [
            pltpu.VMEM(((total + 2) * low, cin), BF16),
            pltpu.VMEM((3, total + 2, ho + 2, wo, cout), BF16),
            pltpu.VMEM((cout, total * high), BF16),
            pltpu.VMEM((cin, total * low), BF16),
            pltpu.VMEM((chunk, cin, cout), F32),
            pltpu.VMEM((chunk, cout, cout), F32),
        ],
    )(*blocks, w1, w2)

    recv = swap(send, "dp", 1)
    own, *sends = call(
        pair_kernel,
        (shape((chunk, tall + short, cout), F32),)
        + tuple(shape((chunk, tall + short, cout), BF16) for _ in range(far_size - 1)),
        "pair",
    )(keep, recv)
    recvs = [swap(value, "dp", hop, 2) for hop, value in enumerate(sends, 1)]
    feature_grad = call(
        lambda *refs: input_grad_kernel(frames, *refs),
        shape((frames * low, cin), BF16),
        "input_grad",
    )(dbox, w1)
    factor = 1.0 / math.sqrt(clips * dp * total * high)
    share = call(
        lambda *refs: sum_kernel(factor, *refs), shape((chunk, tall + short, cout), BF16), "sum"
    )(own, *recvs)
    shares = [share] + [swap(share, "tm", hop) for hop in range(1, tm)]
    one, two = call(
        lambda *refs: spread_kernel(tall, *refs),
        (shape((taps, tall, cout), F32), shape((taps, short, cout), F32)),
        "spread",
    )(*shares)
    return (
        feature_grad.reshape(features.shape),
        one.reshape(3, 3, 3, tall, cout),
        two.reshape(3, 3, 3, short, cout),
    )


def solution(mesh):
    in_specs = (P("dp", "tm", None, None, None), P("dp", "tm", None, None, None), P(), P())
    out_specs = (
        P("dp", "tm", None, None, None),
        P(None, None, None, "dp", None),
        P(None, None, None, "dp", None),
    )
    return jax.shard_map(
        on_device, mesh=mesh, in_specs=in_specs, out_specs=out_specs, check_vma=False
    )
```

```python
import math

import jax
import jax.numpy as jnp
from jax import lax
from jax.experimental import pallas as pl
from jax.experimental.pallas import tpu as pltpu
from jax.sharding import PartitionSpec as P

F32, BF16 = jnp.float32, jnp.bfloat16


def swap(value, axis, hop, stride=1):
    size = lax.axis_size(axis)
    return lax.ppermute(value, axis, [(i, i ^ (hop * stride)) for i in range(size)])


def call(body, out_shape, name, scratch=(), grant=8):
    kernel = pl.pallas_call(
        body,
        out_shape=out_shape,
        scratch_shapes=list(scratch),
        name=name,
        compiler_params=pltpu.CompilerParams(vmem_limit_bytes=grant << 20),
    )
    return lambda *values: kernel(*(pltpu.with_memory_space_constraint(v, pltpu.VMEM) for v in values))


def rows_of(value):
    return value.reshape(-1, value.shape[-1])


def move_down(value, fill_at):
    shape = value.shape
    flat = value.reshape(-1, shape[-2], shape[-1])
    by = 1 if fill_at == 0 else shape[-2] - 1
    turned = pltpu.roll(flat, by, 1)
    place = lax.broadcasted_iota(jnp.int32, turned.shape, 1)
    return jnp.where(place == fill_at, 0.0, turned).reshape(shape)


def pack_kernel(feats_ref, ups_ref, out_ref, wide):
    half = out_ref.shape[-1]
    low = feats_ref.shape[1]
    ins = feats_ref.shape[2] // half
    for part in range(ins):
        out_ref[:, part * low : (part + 1) * low, :] = feats_ref[:, :, part * half : (part + 1) * half]
    frames, ho, wo, _ = ups_ref.shape
    wide[...] = ups_ref[...].reshape(frames * ho, wo, half).astype(F32)
    even = wide[:, pl.ds(0, wo // 2, stride=2), :]
    odd = wide[:, pl.ds(1, wo // 2, stride=2), :]
    both = jnp.concatenate([even, odd], axis=1)
    out_ref[:, ins * low :, :] = both.reshape(frames, ho * wo, half).astype(BF16)


def main_kernel(dims, blocks, w1_ref, w2_ref, keep_ref, send_ref, dbox_ref, xs, uc, ht, ft, g1, g2):
    tm, dp, hi, wi, chunk = dims
    ho, wo = 2 * hi, 2 * wi
    low = hi * wi
    frames = blocks[0].shape[0]
    total = frames * tm
    cin, cout = w1_ref.shape[1], w1_ref.shape[2]
    parts = cin // cout
    me = lax.axis_index("tm")
    mine = lax.axis_index("dp")
    core, far = lax.rem(mine, 2), lax.div(mine, 2)

    xs[: 2 * low] = jnp.zeros((2 * low, cin), BF16)
    uc[:, total:] = jnp.zeros((3, 2) + uc.shape[2:], BF16)
    uc[:, :, 0] = jnp.zeros((3, total + 2) + uc.shape[3:], BF16)
    uc[:, :, ho + 1] = jnp.zeros((3, total + 2) + uc.shape[3:], BF16)
    for hop, block in enumerate(blocks):
        start = (me ^ hop) * frames
        feats = jnp.concatenate(
            [rows_of(block[:, part * low : (part + 1) * low, :]) for part in range(parts)], axis=1
        )
        xs[pl.ds(pl.multiple_of((start + 2) * low, low), frames * low), :] = feats
        ups = block[:, parts * low :, :].reshape(frames, ho, 2, wi, cout)
        wide = ups.astype(F32)
        even, odd = wide[:, :, 0], wide[:, :, 1]
        after = move_down(even, wi - 1)
        before = move_down(odd, 0)
        where = (pl.ds(start, frames), slice(1, ho + 1))
        uc[(0,) + where] = jnp.concatenate([odd, after], axis=2).astype(BF16)
        uc[(1,) + where] = block[:, parts * low :, :].reshape(frames, ho, wo, cout)
        uc[(2,) + where] = jnp.concatenate([before, even], axis=2).astype(BF16)

    by_row = []
    for b in range(3):
        sums = None
        for a in range(3):
            weight = jnp.concatenate([w1_ref[a * 9 + b * 3 + e] for e in range(3)], axis=1)
            term = jnp.dot(xs[a * low : (a + total) * low, :], weight, preferred_element_type=F32)
            sums = term if sums is None else sums + term
        by_row.append(sums.reshape(total, hi, wi, 3 * cout))
    zero = jnp.zeros((total, wi, 3 * cout), F32)
    pre_rows = []
    for row in range(hi):
        up = by_row[0][:, row - 1] if row else zero
        down = by_row[2][:, row + 1] if row + 1 < hi else zero
        pre_rows.append(up + by_row[1][:, row] + by_row[2][:, row])
        pre_rows.append(by_row[0][:, row] + by_row[1][:, row] + down)
    sums = jnp.stack(pre_rows, axis=1)
    first, middle, last = (sums[..., e * cout : (e + 1) * cout] for e in range(3))
    even = move_down(first, 0) + middle + last
    odd = first + middle + move_down(last, wi - 1)
    pre = jnp.concatenate([even, odd], axis=2)
    sigma = 1.0 / (1.0 + jnp.exp(-pre))
    hidden = pre * sigma
    slope = sigma * (1.0 + pre * (1.0 - sigma))
    ht[...] = rows_of(hidden).T.astype(BF16)
    ft[...] = xs[2 * low :, :].astype(F32).T.astype(BF16)

    back = None
    for a in range(3):
        for b in range(3):
            ups = jnp.concatenate(
                [rows_of(uc[e, 2 - a : 2 - a + total, 2 - b : 2 - b + ho]) for e in range(3)], axis=1
            )
            weight = jnp.concatenate([w2_ref[a * 9 + b * 3 + e] for e in range(3)], axis=1)
            term = lax.dot_general(ups, weight, (((1,), (1,)), ((), ())), preferred_element_type=F32)
            back = term if back is None else back + term
    dpre = (back.reshape(slope.shape) * slope).astype(BF16).astype(F32)
    even, odd = dpre[:, :, :wi], dpre[:, :, wi:]
    columns = (odd + move_down(even, wi - 1), even + odd, move_down(odd, 0) + even)
    for e in range(3):
        col = columns[e]
        for b in range(3):
            picked = []
            for row in range(hi):
                one, two = 2 * row + 1 - b, 2 * row + 2 - b
                value = None
                for at in (one, two):
                    if 0 <= at < ho:
                        value = col[:, at] if value is None else value + col[:, at]
                picked.append(value)
            box = jnp.concatenate(picked, axis=1)
            dbox_ref[b * 3 + e, :total] = box.astype(BF16)
    dbox_ref[:, total:] = jnp.zeros((9, 2, low, cout), BF16)

    far_size = dp // 2
    tall, short = cin // dp, cout // dp
    for j in range(chunk):
        tap = jnp.minimum(me * chunk + j, 26)
        a, rest = lax.div(tap, 9), lax.rem(tap, 9)
        b, e = lax.div(rest, 3), lax.rem(rest, 3)
        boxes = rows_of(dbox_ref[rest, pl.ds(2 - a, total)])
        g1[j] = jnp.dot(ft[...], boxes, preferred_element_type=F32)
        ups = rows_of(uc[e, pl.ds(2 - a, total), pl.ds(2 - b, ho)])
        g2[j] = jnp.dot(ht[...], ups, preferred_element_type=F32)
    for hop in range(far_size):
        for ref, side in ((keep_ref, core), (send_ref, 1 - core)):
            at = (far ^ hop) * 2 + side
            ref[hop, :, :tall] = g1[:, pl.ds(pl.multiple_of(at * tall, tall), tall)].astype(ref.dtype)
            ref[hop, :, tall:] = g2[:, pl.ds(pl.multiple_of(at * short, short), short)].astype(ref.dtype)


def input_grad_kernel(frames, dbox_ref, w1_ref, out_ref):
    start = lax.axis_index("tm") * frames
    total = None
    for a in range(3):
        for b in range(3):
            boxes = jnp.concatenate(
                [rows_of(dbox_ref[b * 3 + e, pl.ds(start + 2 - a, frames)]) for e in range(3)], axis=1
            )
            weight = jnp.concatenate([w1_ref[a * 9 + b * 3 + e] for e in range(3)], axis=1)
            term = lax.dot_general(boxes, weight, (((1,), (1,)), ((), ())), preferred_element_type=F32)
            total = term if total is None else total + term
    out_ref[...] = total.astype(BF16)


def pair_kernel(keep_ref, recv_ref, own_ref, *send_refs):
    own_ref[...] = keep_ref[0] + recv_ref[0].astype(F32)
    for hop, ref in enumerate(send_refs, 1):
        ref[...] = (keep_ref[hop] + recv_ref[hop].astype(F32)).astype(BF16)


def sum_kernel(factor, own_ref, *refs):
    *recv_refs, out_ref = refs
    total = own_ref[...]
    for ref in recv_refs:
        total += ref[...].astype(F32)
    out_ref[...] = (total * factor).astype(BF16)


def spread_kernel(tall, *refs):
    *in_refs, one_ref, two_ref = refs
    me = lax.axis_index("tm")
    chunk = in_refs[0].shape[0]
    taps = one_ref.shape[0]
    for hop, ref in enumerate(in_refs):
        for j in range(chunk):
            tap = (me ^ hop) * chunk + j

            @pl.when(tap < taps)
            def _():
                one_ref[tap] = ref[j, :tall].astype(F32)
                two_ref[tap] = ref[j, tall:].astype(F32)


def on_device(features, upstream, weight_one, weight_two):
    clips, frames, hi, wi, cin = features.shape
    ho, wo, cout = upstream.shape[2:]
    tm, dp = lax.axis_size("tm"), lax.axis_size("dp")
    taps = 27
    chunk = -(-taps // tm)
    total = frames * tm
    low, high = hi * wi, ho * wo
    far_size = dp // 2
    tall, short = cin // dp, cout // dp
    shape, near = jax.ShapeDtypeStruct, pltpu.VMEM
    w1 = weight_one.reshape(taps, cin, cout)
    w2 = weight_two.reshape(taps, cout, cout)

    packed = call(
        pack_kernel,
        near((frames, low * (cin // cout) + high, cout), BF16),
        "pack",
        [pltpu.VMEM((frames * ho, wo, cout), F32)],
    )(features.reshape(frames, low, cin), upstream.reshape(frames, ho, wo, cout))
    blocks = [packed] + [swap(packed, "tm", hop) for hop in range(1, tm)]

    def main_body(*refs):
        main_kernel((tm, dp, hi, wi, chunk), refs[:tm], *refs[tm:])

    keep, send, dbox = call(
        main_body,
        (
            near((far_size, chunk, tall + short, cout), F32),
            near((far_size, chunk, tall + short, cout), BF16),
            near((9, total + 2, low, cout), BF16),
        ),
        "main",
        [
            pltpu.VMEM(((total + 2) * low, cin), BF16),
            pltpu.VMEM((3, total + 2, ho + 2, wo, cout), BF16),
            pltpu.VMEM((cout, total * high), BF16),
            pltpu.VMEM((cin, total * low), BF16),
            pltpu.VMEM((chunk, cin, cout), F32),
            pltpu.VMEM((chunk, cout, cout), F32),
        ],
        grant=32,
    )(*blocks, w1, w2)

    recv = swap(send, "dp", 1)
    own, *sends = call(
        pair_kernel,
        (near((chunk, tall + short, cout), F32),)
        + tuple(near((chunk, tall + short, cout), BF16) for _ in range(far_size - 1)),
        "pair",
    )(keep, recv)
    recvs = [swap(value, "dp", hop, 2) for hop, value in enumerate(sends, 1)]
    feature_grad = call(
        lambda *refs: input_grad_kernel(frames, *refs),
        shape((frames * low, cin), BF16),
        "input_grad",
    )(dbox, w1)
    factor = 1.0 / math.sqrt(clips * dp * total * high)
    share = call(
        lambda *refs: sum_kernel(factor, *refs), near((chunk, tall + short, cout), BF16), "sum"
    )(own, *recvs)
    shares = [share] + [swap(share, "tm", hop) for hop in range(1, tm)]
    one, two = call(
        lambda *refs: spread_kernel(tall, *refs),
        (shape((taps, tall, cout), F32), shape((taps, short, cout), F32)),
        "spread",
    )(*shares)
    return (
        feature_grad.reshape(features.shape),
        one.reshape(3, 3, 3, tall, cout),
        two.reshape(3, 3, 3, short, cout),
    )


def solution(mesh):
    in_specs = (P("dp", "tm", None, None, None), P("dp", "tm", None, None, None), P(), P())
    out_specs = (
        P("dp", "tm", None, None, None),
        P(None, None, None, "dp", None),
        P(None, None, None, "dp", None),
    )
    return jax.shard_map(
        on_device, mesh=mesh, in_specs=in_specs, out_specs=out_specs, check_vma=False
    )
```

```python
import math

import jax
import jax.numpy as jnp
from jax import lax
from jax.experimental import pallas as pl
from jax.experimental.pallas import tpu as pltpu
from jax.sharding import PartitionSpec as P


F32, BF16 = jnp.float32, jnp.bfloat16


def swap(value, axis, hop, stride=1):
    size = lax.axis_size(axis)
    return lax.ppermute(value, axis, [(i, i ^ (hop * stride)) for i in range(size)])


def call(body, out_shape, scratch=(), grant=8, far=0):
    options = {"in_specs": [pl.BlockSpec(memory_space=pltpu.HBM)] * far} if far else {}
    kernel = pl.pallas_call(
        body,
        out_shape=out_shape,
        scratch_shapes=list(scratch),
        compiler_params=pltpu.CompilerParams(vmem_limit_bytes=grant << 20),
        **options,
    )
    space = pltpu.HBM if far else pltpu.VMEM
    return lambda *values: kernel(*(pltpu.with_memory_space_constraint(v, space) for v in values))


def rows_of(value):
    return value.reshape(-1, value.shape[-1])


def move_down(value, fill_at):
    shape = value.shape
    flat = value.reshape(-1, shape[-2], shape[-1])
    by = 1 if fill_at == 0 else shape[-2] - 1
    turned = pltpu.roll(flat, by, 1)
    place = lax.broadcasted_iota(jnp.int32, turned.shape, 1)
    return jnp.where(place == fill_at, 0.0, turned).reshape(shape)


def fetch_kernel(count, *refs):
    sources, targets, done = refs[:count], refs[count:-1], refs[-1]
    copies = [pltpu.make_async_copy(*pair, done.at[i]) for i, pair in enumerate(zip(sources, targets))]
    for copy in copies:
        copy.start()
    for copy in copies:
        copy.wait()


def pack_kernel(feats_far, ups_far, out_ref, feats_ref, ups_ref, wide, done):
    fetch_kernel(2, feats_far, ups_far, feats_ref, ups_ref, done)
    half = out_ref.shape[-1]
    low = feats_ref.shape[1]
    ins = feats_ref.shape[2] // half
    for part in range(ins):
        out_ref[:, part * low : (part + 1) * low, :] = feats_ref[:, :, part * half : (part + 1) * half]
    frames, ho, wo, _ = ups_ref.shape
    wide[...] = ups_ref[...].reshape(frames * ho, wo, half).astype(F32)
    even = wide[:, pl.ds(0, wo // 2, stride=2), :]
    odd = wide[:, pl.ds(1, wo // 2, stride=2), :]
    both = jnp.concatenate([even, odd], axis=1)
    out_ref[:, ins * low :, :] = both.reshape(frames, ho * wo, half).astype(BF16)


def main_kernel(dims, blocks, w1_ref, w2_ref, keep_ref, send_ref, dbox_ref, xs, uc, ht, ft, g1, g2):
    tm, dp, hi, wi, chunk = dims
    ho, wo = 2 * hi, 2 * wi
    low = hi * wi
    frames = blocks[0].shape[0]
    total = frames * tm
    cin, cout = w1_ref.shape[1], w1_ref.shape[2]
    parts = cin // cout
    me = lax.axis_index("tm")
    mine = lax.axis_index("dp")
    core, far = lax.rem(mine, 2), lax.div(mine, 2)

    xs[: 2 * low] = jnp.zeros((2 * low, cin), BF16)
    uc[:, total:] = jnp.zeros((3, 2) + uc.shape[2:], BF16)
    uc[:, :, 0] = jnp.zeros((3, total + 2) + uc.shape[3:], BF16)
    uc[:, :, ho + 1] = jnp.zeros((3, total + 2) + uc.shape[3:], BF16)
    for hop, block in enumerate(blocks):
        start = (me ^ hop) * frames
        feats = jnp.concatenate(
            [rows_of(block[:, part * low : (part + 1) * low, :]) for part in range(parts)], axis=1
        )
        xs[pl.ds(pl.multiple_of((start + 2) * low, low), frames * low), :] = feats
        ups = block[:, parts * low :, :].reshape(frames, ho, 2, wi, cout)
        wide = ups.astype(F32)
        even, odd = wide[:, :, 0], wide[:, :, 1]
        after = move_down(even, wi - 1)
        before = move_down(odd, 0)
        where = (pl.ds(start, frames), slice(1, ho + 1))
        uc[(0,) + where] = jnp.concatenate([odd, after], axis=2).astype(BF16)
        uc[(1,) + where] = block[:, parts * low :, :].reshape(frames, ho, wo, cout)
        uc[(2,) + where] = jnp.concatenate([before, even], axis=2).astype(BF16)

    stacked = jnp.concatenate([xs[a * low : (a + total) * low, :] for a in range(3)], axis=1)
    weight = jnp.concatenate(
        [jnp.concatenate([w1_ref[a * 9 + be] for be in range(9)], axis=1) for a in range(3)], axis=0
    )
    sums = jnp.dot(stacked, weight, preferred_element_type=F32).reshape(total, hi, wi, 9 * cout)
    by_row = [sums[..., b * 3 * cout : (b + 1) * 3 * cout] for b in range(3)]
    zero = jnp.zeros((total, wi, 3 * cout), F32)
    pre_rows = []
    for row in range(hi):
        up = by_row[0][:, row - 1] if row else zero
        down = by_row[2][:, row + 1] if row + 1 < hi else zero
        pre_rows.append(up + by_row[1][:, row] + by_row[2][:, row])
        pre_rows.append(by_row[0][:, row] + by_row[1][:, row] + down)
    sums = jnp.stack(pre_rows, axis=1)
    first, middle, last = (sums[..., e * cout : (e + 1) * cout] for e in range(3))
    even = move_down(first, 0) + middle + last
    odd = first + middle + move_down(last, wi - 1)
    pre = jnp.concatenate([even, odd], axis=2)
    sigma = 1.0 / (1.0 + jnp.exp(-pre))
    hidden = pre * sigma
    slope = sigma * (1.0 + pre * (1.0 - sigma))
    ht[...] = rows_of(hidden).T.astype(BF16)
    ft[...] = xs[2 * low :, :].astype(F32).T.astype(BF16)

    ups = jnp.concatenate(
        [rows_of(uc[e, :total, 2 - b : 2 - b + ho]) for b in range(3) for e in range(3)], axis=1
    )
    weight = jnp.concatenate(
        [jnp.concatenate([w2_ref[a * 9 + be] for be in range(9)], axis=1) for a in range(3)], axis=0
    )
    parts_of = lax.dot_general(ups, weight, (((1,), (1,)), ((), ())), preferred_element_type=F32)
    parts_of = parts_of.reshape(total, ho, wo, 3 * cout)
    back = parts_of[..., 2 * cout :]
    for a in range(2):
        lead = 2 - a
        term = parts_of[lead:, ..., a * cout : (a + 1) * cout]
        back += jnp.concatenate([term, jnp.zeros((lead,) + term.shape[1:], F32)], axis=0)
    dpre = (back.reshape(slope.shape) * slope).astype(BF16).astype(F32)
    even, odd = dpre[:, :, :wi], dpre[:, :, wi:]
    columns = (odd + move_down(even, wi - 1), even + odd, move_down(odd, 0) + even)
    for e in range(3):
        col = columns[e]
        for b in range(3):
            picked = []
            for row in range(hi):
                one, two = 2 * row + 1 - b, 2 * row + 2 - b
                value = None
                for at in (one, two):
                    if 0 <= at < ho:
                        value = col[:, at] if value is None else value + col[:, at]
                picked.append(value)
            box = jnp.concatenate(picked, axis=1)
            dbox_ref[b * 3 + e, :total] = box.astype(BF16)
    dbox_ref[:, total:] = jnp.zeros((9, 2, low, cout), BF16)

    far_size = dp // 2
    tall, short = cin // dp, cout // dp
    for j in range(0, chunk, 2):
        boxes, ups = [], []
        for k in range(j, min(j + 2, chunk)):
            tap = jnp.minimum(me * chunk + k, 26)
            a, rest = lax.div(tap, 9), lax.rem(tap, 9)
            b, e = lax.div(rest, 3), lax.rem(rest, 3)
            boxes.append(rows_of(dbox_ref[rest, pl.ds(2 - a, total)]))
            ups.append(rows_of(uc[e, pl.ds(2 - a, total), pl.ds(2 - b, ho)]))
        one = jnp.dot(ft[...], jnp.concatenate(boxes, axis=1), preferred_element_type=F32)
        two = jnp.dot(ht[...], jnp.concatenate(ups, axis=1), preferred_element_type=F32)
        for k in range(len(boxes)):
            g1[j + k] = one[:, k * cout : (k + 1) * cout]
            g2[j + k] = two[:, k * cout : (k + 1) * cout]
    for hop in range(far_size):
        for ref, side in ((keep_ref, core), (send_ref, 1 - core)):
            at = (far ^ hop) * 2 + side
            ref[hop, :, :tall] = g1[:, pl.ds(pl.multiple_of(at * tall, tall), tall)].astype(ref.dtype)
            ref[hop, :, tall:] = g2[:, pl.ds(pl.multiple_of(at * short, short), short)].astype(ref.dtype)


def input_grad_kernel(frames, dbox_ref, w1_ref, out_ref):
    start = lax.axis_index("tm") * frames
    total = None
    for a in range(3):
        for b in range(3):
            boxes = jnp.concatenate(
                [rows_of(dbox_ref[b * 3 + e, pl.ds(start + 2 - a, frames)]) for e in range(3)], axis=1
            )
            weight = jnp.concatenate([w1_ref[a * 9 + b * 3 + e] for e in range(3)], axis=1)
            term = lax.dot_general(boxes, weight, (((1,), (1,)), ((), ())), preferred_element_type=F32)
            total = term if total is None else total + term
    out_ref[...] = total.astype(BF16)


def pair_kernel(keep_ref, recv_ref, own_ref, *send_refs):
    own_ref[...] = keep_ref[0] + recv_ref[0].astype(F32)
    for hop, ref in enumerate(send_refs, 1):
        ref[...] = (keep_ref[hop] + recv_ref[hop].astype(F32)).astype(BF16)


def sum_kernel(factor, own_ref, *refs):
    *recv_refs, out_ref = refs
    total = own_ref[...]
    for ref in recv_refs:
        total += ref[...].astype(F32)
    out_ref[...] = (total * factor).astype(BF16)


def spread_kernel(tall, *refs):
    *in_refs, one_ref, two_ref = refs
    me = lax.axis_index("tm")
    chunk = in_refs[0].shape[0]
    taps = one_ref.shape[0]
    for hop, ref in enumerate(in_refs):
        for j in range(chunk):
            tap = (me ^ hop) * chunk + j

            @pl.when(tap < taps)
            def _():
                one_ref[tap] = ref[j, :tall].astype(F32)
                two_ref[tap] = ref[j, tall:].astype(F32)


def on_device(features, upstream, weight_one, weight_two):
    clips, frames, hi, wi, cin = features.shape
    ho, wo, cout = upstream.shape[2:]
    tm, dp = lax.axis_size("tm"), lax.axis_size("dp")
    taps = 27
    chunk = -(-taps // tm)
    total = frames * tm
    low, high = hi * wi, ho * wo
    far_size = dp // 2
    tall, short = cin // dp, cout // dp
    shape, near = jax.ShapeDtypeStruct, pltpu.VMEM
    w1 = weight_one.reshape(taps, cin, cout)
    w2 = weight_two.reshape(taps, cout, cout)

    packed = call(
        pack_kernel,
        near((frames, low * (cin // cout) + high, cout), BF16),
        [
            pltpu.VMEM((frames, low, cin), BF16),
            pltpu.VMEM((frames, ho, wo, cout), BF16),
            pltpu.VMEM((frames * ho, wo, cout), F32),
            pltpu.SemaphoreType.DMA((2,)),
        ],
        far=2,
    )(features.reshape(frames, low, cin), upstream.reshape(frames, ho, wo, cout))
    blocks = [packed] + [swap(packed, "tm", hop) for hop in range(1, tm)]

    w1, w2 = call(
        lambda *refs: fetch_kernel(2, *refs),
        (near(w1.shape, BF16), near(w2.shape, BF16)),
        [pltpu.SemaphoreType.DMA((2,))],
        far=2,
    )(w1, w2)

    def main_body(*refs):
        main_kernel((tm, dp, hi, wi, chunk), refs[:tm], *refs[tm:])

    keep, send, dbox = call(
        main_body,
        (
            near((far_size, chunk, tall + short, cout), F32),
            near((far_size, chunk, tall + short, cout), BF16),
            near((9, total + 2, low, cout), BF16),
        ),
        [
            pltpu.VMEM(((total + 2) * low, cin), BF16),
            pltpu.VMEM((3, total + 2, ho + 2, wo, cout), BF16),
            pltpu.VMEM((cout, total * high), BF16),
            pltpu.VMEM((cin, total * low), BF16),
            pltpu.VMEM((chunk, cin, cout), F32),
            pltpu.VMEM((chunk, cout, cout), F32),
        ],
        grant=32,
    )(*blocks, w1, w2)

    recv = swap(send, "dp", 1)
    own, *sends = call(
        pair_kernel,
        (near((chunk, tall + short, cout), F32),)
        + tuple(near((chunk, tall + short, cout), BF16) for _ in range(far_size - 1)),
    )(keep, recv)
    recvs = [swap(value, "dp", hop, 2) for hop, value in enumerate(sends, 1)]
    feature_grad = call(lambda *refs: input_grad_kernel(frames, *refs), shape((frames * low, cin), BF16))(dbox, w1)
    factor = 1.0 / math.sqrt(clips * dp * total * high)
    share = call(lambda *refs: sum_kernel(factor, *refs), near((chunk, tall + short, cout), BF16))(own, *recvs)
    shares = [share] + [swap(share, "tm", hop) for hop in range(1, tm)]
    one, two = call(
        lambda *refs: spread_kernel(tall, *refs), (shape((taps, tall, cout), F32), shape((taps, short, cout), F32))
    )(*shares)
    return (
        feature_grad.reshape(features.shape),
        one.reshape(3, 3, 3, tall, cout),
        two.reshape(3, 3, 3, short, cout),
    )


def solution(mesh):
    in_specs = (P("dp", "tm", None, None, None), P("dp", "tm", None, None, None), P(), P())
    out_specs = (
        P("dp", "tm", None, None, None),
        P(None, None, None, "dp", None),
        P(None, None, None, "dp", None),
    )
    return jax.shard_map(
        on_device, mesh=mesh, in_specs=in_specs, out_specs=out_specs, check_vma=False
    )
```

```python
import math

import jax
import jax.numpy as jnp
from jax import lax
from jax.experimental import pallas as pl
from jax.experimental.pallas import tpu as pltpu
from jax.sharding import PartitionSpec as P


F32, BF16 = jnp.float32, jnp.bfloat16


def swap(value, axis, hop, stride=1):
    size = lax.axis_size(axis)
    return lax.ppermute(value, axis, [(i, i ^ (hop * stride)) for i in range(size)])


def call(body, out_shape, scratch=(), grant=8, far=0):
    options = {"in_specs": [pl.BlockSpec(memory_space=pltpu.HBM)] * far} if far else {}
    kernel = pl.pallas_call(
        body,
        out_shape=out_shape,
        scratch_shapes=list(scratch),
        compiler_params=pltpu.CompilerParams(vmem_limit_bytes=grant << 20),
        **options,
    )
    space = pltpu.HBM if far else pltpu.VMEM
    return lambda *values: kernel(*(pltpu.with_memory_space_constraint(v, space) for v in values))


def rows_of(value):
    return value.reshape(-1, value.shape[-1])


def move_down(value, fill_at):
    shape = value.shape
    flat = value.reshape(-1, shape[-2], shape[-1])
    by = 1 if fill_at == 0 else shape[-2] - 1
    turned = pltpu.roll(flat, by, 1)
    place = lax.broadcasted_iota(jnp.int32, turned.shape, 1)
    return jnp.where(place == fill_at, 0.0, turned).reshape(shape)


def fetch_kernel(count, *refs):
    sources, targets, done = refs[:count], refs[count:-1], refs[-1]
    copies = [pltpu.make_async_copy(*pair, done.at[i]) for i, pair in enumerate(zip(sources, targets))]
    for copy in copies:
        copy.start()
    for copy in copies:
        copy.wait()


def pack_kernel(feats_far, ups_far, out_ref, feats_ref, ups_ref, wide, done):
    fetch_kernel(2, feats_far, ups_far, feats_ref, ups_ref, done)
    half = out_ref.shape[-1]
    low = feats_ref.shape[1]
    ins = feats_ref.shape[2] // half
    for part in range(ins):
        out_ref[:, part * low : (part + 1) * low, :] = feats_ref[:, :, part * half : (part + 1) * half]
    frames, ho, wo, _ = ups_ref.shape
    wide[...] = ups_ref[...].reshape(frames * ho, wo, half).astype(F32)
    even = wide[:, pl.ds(0, wo // 2, stride=2), :]
    odd = wide[:, pl.ds(1, wo // 2, stride=2), :]
    both = jnp.concatenate([even, odd], axis=1)
    out_ref[:, ins * low :, :] = both.reshape(frames, ho * wo, half).astype(BF16)


def shifted(block, skip, ho, wi):
    frames, _, cout = block.shape
    ups = block[:, skip:, :]
    wide = ups.reshape(frames, ho, 2, wi, cout).astype(F32)
    even, odd = wide[:, :, 0], wide[:, :, 1]
    after = move_down(even, wi - 1)
    before = move_down(odd, 0)
    return (
        jnp.concatenate([odd, after], axis=2).astype(BF16),
        ups.reshape(frames, ho, 2 * wi, cout),
        jnp.concatenate([before, even], axis=2).astype(BF16),
    )


def clear_edges(uc):
    rows = uc.shape[2]
    for row in (0, rows - 1):
        uc[:, :, row] = jnp.zeros(uc.shape[:2] + uc.shape[3:], BF16)


def through_second(uc, starts, frames, w2_ref):
    ho = uc.shape[2] - 2
    ups = jnp.concatenate(
        [
            jnp.concatenate([rows_of(uc[e, pl.ds(start, frames), 2 - b : 2 - b + ho]) for start in starts], axis=0)
            for b in range(3)
            for e in range(3)
        ],
        axis=1,
    )
    weight = jnp.concatenate(
        [jnp.concatenate([w2_ref[a * 9 + be] for be in range(9)], axis=1) for a in range(3)], axis=0
    )
    return lax.dot_general(ups, weight, (((1,), (1,)), ((), ())), preferred_element_type=F32)


def early_kernel(dims, one, two, w2_ref, out_ref, uc):
    hi, wi, skip = dims
    frames = one.shape[0]
    clear_edges(uc)
    for at, block in enumerate((one, two)):
        for e, value in enumerate(shifted(block, skip, 2 * hi, wi)):
            uc[e, at * frames : (at + 1) * frames, 1 : 2 * hi + 1] = value
    out_ref[...] = through_second(uc, [0], 2 * frames, w2_ref)


def kernel_grads(dims, same_core, ft, ht, uc, dbox_ref, out_ref):
    _, dp, hi, _, chunk = dims
    me, mine = lax.axis_index("tm"), lax.axis_index("dp")
    core, far = lax.rem(mine, 2), lax.div(mine, 2)
    side = core if same_core else 1 - core
    total, ho = dbox_ref.shape[1] - 2, 2 * hi
    cout = dbox_ref.shape[-1]
    tall, short = ft.shape[1], ht.shape[1]
    hops = range(dp // 2)

    def picked(ref):
        return jnp.concatenate([ref[(far ^ hop) * 2 + side] for hop in hops], axis=0).astype(BF16)

    wide, narrow = picked(ft), picked(ht)
    taps = []
    for j in range(chunk):
        tap = jnp.minimum(me * chunk + j, 26)
        rest = lax.rem(tap, 9)
        taps.append((lax.div(tap, 9), lax.div(rest, 3), lax.rem(rest, 3)))
    for j in range(0, chunk, 2):
        wanted = taps[j : j + 2]
        ups = [rows_of(uc[e, pl.ds(2 - a, total), pl.ds(2 - b, ho)]) for a, b, e in wanted]
        two = jnp.dot(narrow, jnp.concatenate(ups, axis=1), preferred_element_type=F32)
        for hop in hops:
            for k in range(len(wanted)):
                part = two[hop * short : (hop + 1) * short, k * cout : (k + 1) * cout]
                out_ref[hop, j + k, tall:] = part.astype(out_ref.dtype)
    for j in range(0, chunk, 2):
        wanted = taps[j : j + 2]
        boxes = [rows_of(dbox_ref[b * 3 + e, pl.ds(2 - a, total)]) for a, b, e in wanted]
        one = jnp.dot(wide, jnp.concatenate(boxes, axis=1), preferred_element_type=F32)
        for hop in hops:
            for k in range(len(wanted)):
                part = one[hop * tall : (hop + 1) * tall, k * cout : (k + 1) * cout]
                out_ref[hop, j + k, :tall] = part.astype(out_ref.dtype)


def main_kernel(dims, blocks, w1_ref, w2_ref, early_ref, send_ref, ft, ht, uc, dbox_ref, xs, zs):
    tm, _, hi, wi, _ = dims
    ho, wo = 2 * hi, 2 * wi
    low = hi * wi
    frames = blocks[0].shape[0]
    total = frames * tm
    cin, cout = w1_ref.shape[1], w1_ref.shape[2]
    parts = cin // cout
    me = lax.axis_index("tm")

    xs[: 2 * low] = jnp.zeros((2 * low, cin), BF16)
    uc[:, total:] = jnp.zeros((3, 2) + uc.shape[2:], BF16)
    clear_edges(uc)
    starts = [(me ^ hop) * frames for hop in range(tm)]
    for start, block in zip(starts, blocks):
        feats = jnp.concatenate(
            [rows_of(block[:, part * low : (part + 1) * low, :]) for part in range(parts)], axis=1
        )
        xs[pl.ds(pl.multiple_of((start + 2) * low, low), frames * low), :] = feats
        for e, value in enumerate(shifted(block, parts * low, ho, wi)):
            uc[e, pl.ds(start, frames), 1 : ho + 1] = value

    stacked = jnp.concatenate([xs[a * low : (a + total) * low, :] for a in range(3)], axis=1)
    weight = jnp.concatenate(
        [jnp.concatenate([w1_ref[a * 9 + be] for be in range(9)], axis=1) for a in range(3)], axis=0
    )
    sums = jnp.dot(stacked, weight, preferred_element_type=F32).reshape(total, hi, wi, 9 * cout)
    by_row = [sums[..., b * 3 * cout : (b + 1) * 3 * cout] for b in range(3)]
    zero = jnp.zeros((total, wi, 3 * cout), F32)
    pre_rows = []
    for row in range(hi):
        up = by_row[0][:, row - 1] if row else zero
        down = by_row[2][:, row + 1] if row + 1 < hi else zero
        pre_rows.append(up + by_row[1][:, row] + by_row[2][:, row])
        pre_rows.append(by_row[0][:, row] + by_row[1][:, row] + down)
    sums = jnp.stack(pre_rows, axis=1)
    first, middle, last = (sums[..., e * cout : (e + 1) * cout] for e in range(3))
    even = move_down(first, 0) + middle + last
    odd = first + middle + move_down(last, wi - 1)
    pre = jnp.concatenate([even, odd], axis=2)
    sigma = 1.0 / (1.0 + jnp.exp(-pre))
    hidden = pre * sigma
    slope = sigma * (1.0 + pre * (1.0 - sigma))
    ht[...] = rows_of(hidden).T.reshape(ht.shape)
    ft[...] = xs[2 * low :, :].astype(F32).T.reshape(ft.shape)

    late = starts[1:-1]
    for found, places in ((through_second(uc, late, frames, w2_ref), late), (early_ref[...], starts[:: tm - 1])):
        found = found.reshape(len(places), frames, ho, wo, 3 * cout)
        for at, start in enumerate(places):
            zs[pl.ds(start, frames)] = found[at]
    parts_of = zs[...]
    back = parts_of[..., 2 * cout :]
    for a in range(2):
        lead = 2 - a
        term = parts_of[lead:, ..., a * cout : (a + 1) * cout]
        back += jnp.concatenate([term, jnp.zeros((lead,) + term.shape[1:], F32)], axis=0)
    dpre = (back.reshape(slope.shape) * slope).astype(BF16).astype(F32)
    even, odd = dpre[:, :, :wi], dpre[:, :, wi:]
    columns = (odd + move_down(even, wi - 1), even + odd, move_down(odd, 0) + even)
    for e in range(3):
        col = columns[e]
        for b in range(3):
            picked = []
            for row in range(hi):
                one, two = 2 * row + 1 - b, 2 * row + 2 - b
                value = None
                for at in (one, two):
                    if 0 <= at < ho:
                        value = col[:, at] if value is None else value + col[:, at]
                picked.append(value)
            box = jnp.concatenate(picked, axis=1)
            dbox_ref[b * 3 + e, :total] = box.astype(BF16)
    dbox_ref[:, total:] = jnp.zeros((9, 2, low, cout), BF16)

    kernel_grads(dims, False, ft, ht, uc, dbox_ref, send_ref)


def input_grad_kernel(frames, dbox_ref, w1_ref, out_ref):
    start = lax.axis_index("tm") * frames
    total = None
    for a in range(3):
        for b in range(3):
            boxes = jnp.concatenate(
                [rows_of(dbox_ref[b * 3 + e, pl.ds(start + 2 - a, frames)]) for e in range(3)], axis=1
            )
            weight = jnp.concatenate([w1_ref[a * 9 + b * 3 + e] for e in range(3)], axis=1)
            term = lax.dot_general(boxes, weight, (((1,), (1,)), ((), ())), preferred_element_type=F32)
            total = term if total is None else total + term
    out_ref[...] = total.astype(BF16)


def pair_kernel(keep_ref, recv_ref, own_ref, *send_refs):
    own_ref[...] = keep_ref[0] + recv_ref[0].astype(F32)
    for hop, ref in enumerate(send_refs, 1):
        ref[...] = (keep_ref[hop] + recv_ref[hop].astype(F32)).astype(BF16)


def sum_kernel(factor, own_ref, *refs):
    *recv_refs, out_ref = refs
    total = own_ref[...]
    for ref in recv_refs:
        total += ref[...].astype(F32)
    out_ref[...] = (total * factor).astype(BF16)


def spread_kernel(tall, *refs):
    *in_refs, one_ref, two_ref = refs
    me = lax.axis_index("tm")
    chunk = in_refs[0].shape[0]
    taps = one_ref.shape[0]
    for hop, ref in enumerate(in_refs):
        for j in range(chunk):
            tap = (me ^ hop) * chunk + j

            @pl.when(tap < taps)
            def _():
                one_ref[tap] = ref[j, :tall].astype(F32)
                two_ref[tap] = ref[j, tall:].astype(F32)


def on_device(features, upstream, weight_one, weight_two):
    clips, frames, hi, wi, cin = features.shape
    ho, wo, cout = upstream.shape[2:]
    tm, dp = lax.axis_size("tm"), lax.axis_size("dp")
    taps = 27
    chunk = -(-taps // tm)
    total = frames * tm
    low, high = hi * wi, ho * wo
    far_size = dp // 2
    tall, short = cin // dp, cout // dp
    shape, near = jax.ShapeDtypeStruct, pltpu.VMEM
    w1 = weight_one.reshape(taps, cin, cout)
    w2 = weight_two.reshape(taps, cout, cout)

    packed = call(
        pack_kernel,
        near((frames, low * (cin // cout) + high, cout), BF16),
        [
            pltpu.VMEM((frames, low, cin), BF16),
            pltpu.VMEM((frames, ho, wo, cout), BF16),
            pltpu.VMEM((frames * ho, wo, cout), F32),
            pltpu.SemaphoreType.DMA((2,)),
        ],
        far=2,
    )(features.reshape(frames, low, cin), upstream.reshape(frames, ho, wo, cout))
    blocks = [packed] + [swap(packed, "tm", hop) for hop in range(1, tm)]

    w1, w2 = call(
        lambda *refs: fetch_kernel(2, *refs),
        (near(w1.shape, BF16), near(w2.shape, BF16)),
        [pltpu.SemaphoreType.DMA((2,))],
        far=2,
    )(w1, w2)

    early = call(
        lambda *refs: early_kernel((hi, wi, low * (cin // cout)), *refs),
        near((2 * frames * high, 3 * cout), F32),
        [pltpu.VMEM((3, 2 * frames, ho + 2, wo, cout), BF16)],
    )(blocks[0], blocks[-1], w2)

    def main_body(*refs):
        main_kernel((tm, dp, hi, wi, chunk), refs[:tm], *refs[tm:])

    send, *held = call(
        main_body,
        (
            near((far_size, chunk, tall + short, cout), BF16),
            near((dp, tall, total * low), F32),
            near((dp, short, total * high), F32),
            near((3, total + 2, ho + 2, wo, cout), BF16),
            near((9, total + 2, low, cout), BF16),
        ),
        [
            pltpu.VMEM(((total + 2) * low, cin), BF16),
            pltpu.VMEM((total, ho, wo, 3 * cout), F32),
        ],
        grant=32,
    )(*blocks, w1, w2, early)
    dbox = held[-1]

    keep = call(
        lambda *refs: kernel_grads((tm, dp, hi, wi, chunk), True, *refs),
        near((far_size, chunk, tall + short, cout), F32),
    )(*held)
    recv = swap(send, "dp", 1)
    own, *sends = call(
        pair_kernel,
        (near((chunk, tall + short, cout), F32),)
        + tuple(near((chunk, tall + short, cout), BF16) for _ in range(far_size - 1)),
    )(keep, recv)
    recvs = [swap(value, "dp", hop, 2) for hop, value in enumerate(sends, 1)]
    feature_grad = call(lambda *refs: input_grad_kernel(frames, *refs), shape((frames * low, cin), BF16))(dbox, w1)
    factor = 1.0 / math.sqrt(clips * dp * total * high)
    share = call(lambda *refs: sum_kernel(factor, *refs), near((chunk, tall + short, cout), BF16))(own, *recvs)
    shares = [share] + [swap(share, "tm", hop) for hop in range(1, tm)]
    one, two = call(
        lambda *refs: spread_kernel(tall, *refs), (shape((taps, tall, cout), F32), shape((taps, short, cout), F32))
    )(*shares)
    return (
        feature_grad.reshape(features.shape),
        one.reshape(3, 3, 3, tall, cout),
        two.reshape(3, 3, 3, short, cout),
    )


def solution(mesh):
    in_specs = (P("dp", "tm", None, None, None), P("dp", "tm", None, None, None), P(), P())
    out_specs = (
        P("dp", "tm", None, None, None),
        P(None, None, None, "dp", None),
        P(None, None, None, "dp", None),
    )
    return jax.shard_map(
        on_device, mesh=mesh, in_specs=in_specs, out_specs=out_specs, check_vma=False
    )
```

```python
import math

import jax
import jax.numpy as jnp
from jax import lax
from jax.experimental import pallas as pl
from jax.experimental.pallas import tpu as pltpu
from jax.sharding import PartitionSpec as P


F32, BF16 = jnp.float32, jnp.bfloat16


def swap(value, axis, hop, stride=1):
    size = lax.axis_size(axis)
    return lax.ppermute(value, axis, [(i, i ^ (hop * stride)) for i in range(size)])


def call(body, out_shape, scratch=(), grant=8, far=0, alias=None):
    options = {"in_specs": [pl.BlockSpec(memory_space=pltpu.HBM)] * far} if far else {}
    kernel = pl.pallas_call(
        body,
        out_shape=out_shape,
        scratch_shapes=list(scratch),
        input_output_aliases=alias or {},
        compiler_params=pltpu.CompilerParams(vmem_limit_bytes=grant << 20),
        **options,
    )
    space = pltpu.HBM if far else pltpu.VMEM
    return lambda *values: kernel(*(pltpu.with_memory_space_constraint(v, space) for v in values))


def rows_of(value):
    return value.reshape(-1, value.shape[-1])


def move_down(value, fill_at):
    shape = value.shape
    flat = value.reshape(-1, shape[-2], shape[-1])
    by = 1 if fill_at == 0 else shape[-2] - 1
    turned = pltpu.roll(flat, by, 1)
    place = lax.broadcasted_iota(jnp.int32, turned.shape, 1)
    return jnp.where(place == fill_at, 0.0, turned).reshape(shape)


def fetch_kernel(count, *refs):
    sources, targets, done = refs[:count], refs[count:-1], refs[-1]
    copies = [pltpu.make_async_copy(*pair, done.at[i]) for i, pair in enumerate(zip(sources, targets))]
    for copy in copies:
        copy.start()
    for copy in copies:
        copy.wait()


def pack_kernel(feats_far, ups_far, out_ref, feats_ref, ups_ref, wide, done):
    fetch_kernel(2, feats_far, ups_far, feats_ref, ups_ref, done)
    half = out_ref.shape[-1]
    low = feats_ref.shape[1]
    ins = feats_ref.shape[2] // half
    for part in range(ins):
        out_ref[:, part * low : (part + 1) * low, :] = feats_ref[:, :, part * half : (part + 1) * half]
    frames, ho, wo, _ = ups_ref.shape
    wide[...] = ups_ref[...].reshape(frames * ho, wo, half).astype(F32)
    even = wide[:, pl.ds(0, wo // 2, stride=2), :]
    odd = wide[:, pl.ds(1, wo // 2, stride=2), :]
    both = jnp.concatenate([even, odd], axis=1)
    out_ref[:, ins * low :, :] = both.reshape(frames, ho * wo, half).astype(BF16)


def shifted(block, skip, ho, wi):
    frames, _, cout = block.shape
    ups = block[:, skip:, :]
    wide = ups.reshape(frames, ho, 2, wi, cout).astype(F32)
    even, odd = wide[:, :, 0], wide[:, :, 1]
    after = move_down(even, wi - 1)
    before = move_down(odd, 0)
    return (
        jnp.concatenate([odd, after], axis=2).astype(BF16),
        ups.reshape(frames, ho, 2 * wi, cout),
        jnp.concatenate([before, even], axis=2).astype(BF16),
    )


def clear_edges(uc):
    rows = uc.shape[2]
    for row in (0, rows - 1):
        uc[:, :, row] = jnp.zeros(uc.shape[:2] + uc.shape[3:], BF16)


def through_second(uc, starts, frames, w2_ref):
    ho = uc.shape[2] - 2
    ups = jnp.concatenate(
        [
            jnp.concatenate([rows_of(uc[e, pl.ds(start, frames), 2 - b : 2 - b + ho]) for start in starts], axis=0)
            for b in range(3)
            for e in range(3)
        ],
        axis=1,
    )
    weight = jnp.concatenate(
        [jnp.concatenate([w2_ref[a * 9 + be] for be in range(9)], axis=1) for a in range(3)], axis=0
    )
    return lax.dot_general(ups, weight, (((1,), (1,)), ((), ())), preferred_element_type=F32)


def place(dims, hop, block, xs, uc):
    _, hi, wi, parts = dims
    frames, _, _ = block.shape
    low = hi * wi
    start = (lax.axis_index("tm") ^ hop) * frames
    feats = jnp.concatenate([rows_of(block[:, part * low : (part + 1) * low, :]) for part in range(parts)], axis=1)
    xs[pl.ds(pl.multiple_of((start + 2) * low, low), frames * low), :] = feats
    for e, value in enumerate(shifted(block, parts * low, 2 * hi, wi)):
        uc[e, pl.ds(start, frames), 1 : 2 * hi + 1] = value
    return start


def add_second(starts, frames, w2_ref, uc, zs):
    found = through_second(uc, starts, frames, w2_ref).reshape((len(starts), frames) + zs.shape[1:])
    for at, start in enumerate(starts):
        zs[pl.ds(start, frames)] = found[at]


def early_kernel(dims, one, two, w2_ref, zs, uc, xs):
    tm, hi, wi, _ = dims
    total, low = zs.shape[0], hi * wi
    xs[: 2 * low] = jnp.zeros((2 * low, xs.shape[1]), BF16)
    uc[:, total:] = jnp.zeros((3, 2) + uc.shape[2:], BF16)
    clear_edges(uc)
    starts = [place(dims, hop, block, xs, uc) for hop, block in ((0, one), (tm - 1, two))]
    add_second(starts, one.shape[0], w2_ref, uc, zs)


def kernel_grads(dims, same_core, ft, ht, uc, dbox_ref, out_ref):
    _, dp, hi, _, chunk = dims
    me, mine = lax.axis_index("tm"), lax.axis_index("dp")
    core, far = lax.rem(mine, 2), lax.div(mine, 2)
    side = core if same_core else 1 - core
    total, ho = dbox_ref.shape[1] - 2, 2 * hi
    cout = dbox_ref.shape[-1]
    tall, short = ft.shape[1], ht.shape[1]
    hops = range(dp // 2)

    def picked(ref):
        return jnp.concatenate([ref[(far ^ hop) * 2 + side] for hop in hops], axis=0).astype(BF16)

    wide, narrow = picked(ft), picked(ht)
    taps = []
    for j in range(chunk):
        tap = jnp.minimum(me * chunk + j, 26)
        rest = lax.rem(tap, 9)
        taps.append((lax.div(tap, 9), lax.div(rest, 3), lax.rem(rest, 3)))
    for j in range(0, chunk, 2):
        wanted = taps[j : j + 2]
        ups = [rows_of(uc[e, pl.ds(2 - a, total), pl.ds(2 - b, ho)]) for a, b, e in wanted]
        two = jnp.dot(narrow, jnp.concatenate(ups, axis=1), preferred_element_type=F32)
        for hop in hops:
            for k in range(len(wanted)):
                part = two[hop * short : (hop + 1) * short, k * cout : (k + 1) * cout]
                out_ref[hop, j + k, tall:] = part.astype(out_ref.dtype)
    for j in range(0, chunk, 2):
        wanted = taps[j : j + 2]
        boxes = [rows_of(dbox_ref[b * 3 + e, pl.ds(2 - a, total)]) for a, b, e in wanted]
        one = jnp.dot(wide, jnp.concatenate(boxes, axis=1), preferred_element_type=F32)
        for hop in hops:
            for k in range(len(wanted)):
                part = one[hop * tall : (hop + 1) * tall, k * cout : (k + 1) * cout]
                out_ref[hop, j + k, :tall] = part.astype(out_ref.dtype)


def main_kernel(dims, blocks, w1_ref, w2_ref, send_ref, ft, ht, dbox_ref, zs, uc, xs, sums, slopes):
    tm, _, hi, wi, _ = dims
    ho, wo = 2 * hi, 2 * wi
    low = hi * wi
    total = zs.shape[0]
    cin, cout = w1_ref.shape[1], w1_ref.shape[2]
    starts = [place((tm, hi, wi, cin // cout), hop, block, xs, uc) for hop, block in enumerate(blocks, 1)]

    stacked = jnp.concatenate([xs[a * low : (a + total) * low, :] for a in range(3)], axis=1)
    weight = jnp.concatenate(
        [jnp.concatenate([w1_ref[a * 9 + be] for be in range(9)], axis=1) for a in range(3)], axis=0
    )
    sums[...] = jnp.dot(stacked, weight, preferred_element_type=F32).reshape(sums.shape)
    zero = jnp.zeros((wi, 3 * cout), F32)
    group = 128 // (ho * wo)
    for t in range(0, total, group):
        hidden = []
        for at in range(t, t + group):
            by_row = [
                [sums[at, row, :, b * 3 * cout : (b + 1) * 3 * cout] for row in range(hi)] for b in range(3)
            ]
            pre_rows = []
            for row in range(hi):
                up = by_row[0][row - 1] if row else zero
                down = by_row[2][row + 1] if row + 1 < hi else zero
                pre_rows.append(up + by_row[1][row] + by_row[2][row])
                pre_rows.append(by_row[0][row] + by_row[1][row] + down)
            rows = jnp.stack(pre_rows, axis=0)
            first, middle, last = (rows[..., e * cout : (e + 1) * cout] for e in range(3))
            even = move_down(first, 0) + middle + last
            odd = first + middle + move_down(last, wi - 1)
            pre = jnp.concatenate([even, odd], axis=1)
            sigma = 1.0 / (1.0 + jnp.exp(-pre))
            hidden.append(rows_of(pre * sigma))
            slopes[at] = sigma * (1.0 + pre * (1.0 - sigma))
        turned = jnp.concatenate(hidden, axis=0).T
        ht[:, :, t * ho * wo : (t + group) * ho * wo] = turned.reshape(ht.shape[:2] + turned.shape[1:])
    ft[...] = xs[2 * low :, :].astype(F32).T.reshape(ft.shape)

    add_second(starts, blocks[0].shape[0], w2_ref, uc, zs)
    for t in range(total):
        back = zs[t, :, :, 2 * cout :]
        for a in range(2):
            if t + 2 - a < total:
                back += zs[t + 2 - a, :, :, a * cout : (a + 1) * cout]
        dpre = (back * slopes[t]).astype(BF16).astype(F32)
        even, odd = dpre[:, :wi], dpre[:, wi:]
        columns = (odd + move_down(even, wi - 1), even + odd, move_down(odd, 0) + even)
        for e, col in enumerate(columns):
            for b in range(3):
                picked = []
                for row in range(hi):
                    near = [col[at] for at in (2 * row + 1 - b, 2 * row + 2 - b) if 0 <= at < ho]
                    picked.append(sum(near[1:], near[0]))
                dbox_ref[b * 3 + e, t] = jnp.concatenate(picked, axis=0).astype(BF16)
    dbox_ref[:, total:] = jnp.zeros((9, 2, low, cout), BF16)

    kernel_grads(dims, False, ft, ht, uc, dbox_ref, send_ref)


def input_grad_kernel(frames, dbox_ref, w1_ref, out_ref):
    start = lax.axis_index("tm") * frames
    total = None
    for a in range(3):
        for b in range(3):
            boxes = jnp.concatenate(
                [rows_of(dbox_ref[b * 3 + e, pl.ds(start + 2 - a, frames)]) for e in range(3)], axis=1
            )
            weight = jnp.concatenate([w1_ref[a * 9 + b * 3 + e] for e in range(3)], axis=1)
            term = lax.dot_general(boxes, weight, (((1,), (1,)), ((), ())), preferred_element_type=F32)
            total = term if total is None else total + term
    out_ref[...] = total.astype(BF16)


def pair_kernel(keep_ref, recv_ref, own_ref, *send_refs):
    own_ref[...] = keep_ref[0] + recv_ref[0].astype(F32)
    for hop, ref in enumerate(send_refs, 1):
        ref[...] = (keep_ref[hop] + recv_ref[hop].astype(F32)).astype(BF16)


def sum_kernel(factor, own_ref, *refs):
    *recv_refs, out_ref = refs
    total = own_ref[...]
    for ref in recv_refs:
        total += ref[...].astype(F32)
    out_ref[...] = (total * factor).astype(BF16)


def spread_kernel(tall, *refs):
    *in_refs, one_ref, two_ref = refs
    me = lax.axis_index("tm")
    chunk = in_refs[0].shape[0]
    taps = one_ref.shape[0]
    for hop, ref in enumerate(in_refs):
        for j in range(chunk):
            tap = (me ^ hop) * chunk + j

            @pl.when(tap < taps)
            def _():
                one_ref[tap] = ref[j, :tall].astype(F32)
                two_ref[tap] = ref[j, tall:].astype(F32)


def on_device(features, upstream, weight_one, weight_two):
    clips, frames, hi, wi, cin = features.shape
    ho, wo, cout = upstream.shape[2:]
    tm, dp = lax.axis_size("tm"), lax.axis_size("dp")
    taps = 27
    chunk = -(-taps // tm)
    total = frames * tm
    low, high = hi * wi, ho * wo
    far_size = dp // 2
    tall, short = cin // dp, cout // dp
    shape, near = jax.ShapeDtypeStruct, pltpu.VMEM
    w1 = weight_one.reshape(taps, cin, cout)
    w2 = weight_two.reshape(taps, cout, cout)

    packed = call(
        pack_kernel,
        near((frames, low * (cin // cout) + high, cout), BF16),
        [
            pltpu.VMEM((frames, low, cin), BF16),
            pltpu.VMEM((frames, ho, wo, cout), BF16),
            pltpu.VMEM((frames * ho, wo, cout), F32),
            pltpu.SemaphoreType.DMA((2,)),
        ],
        far=2,
    )(features.reshape(frames, low, cin), upstream.reshape(frames, ho, wo, cout))
    blocks = [packed] + [swap(packed, "tm", hop) for hop in range(1, tm)]

    w1, w2 = call(
        lambda *refs: fetch_kernel(2, *refs),
        (near(w1.shape, BF16), near(w2.shape, BF16)),
        [pltpu.SemaphoreType.DMA((2,))],
        far=2,
    )(w1, w2)

    shared = (
        near((total, ho, wo, 3 * cout), F32),
        near((3, total + 2, ho + 2, wo, cout), BF16),
        near(((total + 2) * low, cin), BF16),
    )
    early = call(
        lambda *refs: early_kernel((tm, hi, wi, cin // cout), *refs), shared, grant=12
    )(blocks[0], blocks[-1], w2)

    def main_body(*refs):
        late = tm - 2
        main_kernel((tm, dp, hi, wi, chunk), refs[:late], *refs[late : late + 2], *refs[late + 5 :])

    send, ft, ht, dbox, _, held, _ = call(
        main_body,
        (
            near((far_size, chunk, tall + short, cout), BF16),
            near((dp, tall, total * low), F32),
            near((dp, short, total * high), F32),
            near((9, total + 2, low, cout), BF16),
        )
        + shared,
        [
            pltpu.VMEM((total, hi, wi, 9 * cout), F32),
            pltpu.VMEM((total, ho, wo, cout), F32),
        ],
        grant=32,
        alias={tm: 4, tm + 1: 5, tm + 2: 6},
    )(*blocks[1:-1], w1, w2, *early)

    keep = call(
        lambda *refs: kernel_grads((tm, dp, hi, wi, chunk), True, *refs),
        near((far_size, chunk, tall + short, cout), F32),
    )(ft, ht, held, dbox)
    recv = swap(send, "dp", 1)
    own, *sends = call(
        pair_kernel,
        (near((chunk, tall + short, cout), F32),)
        + tuple(near((chunk, tall + short, cout), BF16) for _ in range(far_size - 1)),
    )(keep, recv)
    recvs = [swap(value, "dp", hop, 2) for hop, value in enumerate(sends, 1)]
    feature_grad = call(lambda *refs: input_grad_kernel(frames, *refs), shape((frames * low, cin), BF16))(dbox, w1)
    factor = 1.0 / math.sqrt(clips * dp * total * high)
    share = call(lambda *refs: sum_kernel(factor, *refs), near((chunk, tall + short, cout), BF16))(own, *recvs)
    shares = [share] + [swap(share, "tm", hop) for hop in range(1, tm)]
    one, two = call(
        lambda *refs: spread_kernel(tall, *refs), (shape((taps, tall, cout), F32), shape((taps, short, cout), F32))
    )(*shares)
    return (
        feature_grad.reshape(features.shape),
        one.reshape(3, 3, 3, tall, cout),
        two.reshape(3, 3, 3, short, cout),
    )


def solution(mesh):
    in_specs = (P("dp", "tm", None, None, None), P("dp", "tm", None, None, None), P(), P())
    out_specs = (
        P("dp", "tm", None, None, None),
        P(None, None, None, "dp", None),
        P(None, None, None, "dp", None),
    )
    return jax.shard_map(
        on_device, mesh=mesh, in_specs=in_specs, out_specs=out_specs, check_vma=False
    )
```
